32 devices in a mesh: rep: 2 (over x), sp: 16 (over z, y, core).
Axes of the slice: x: 2, y: 2, z: 4, core: 2. Of those that a mesh axis runs over, the one named last changes fastest.
Arguments:
- volume: bfloat16 [128, 16, 16, 128], P(('rep', 'sp')), parts along dimension 0, may hold values from -6 to 6
- first_kernel: bfloat16 [3, 3, 3, 128, 128], replicated, may hold values from -0.15625 to 0.15625
- second_kernel: bfloat16 [3, 3, 3, 128, 256], replicated, may hold values from -0.15625 to 0.15625
- deep_kernel: bfloat16 [3, 3, 3, 256, 512], P(None, None, None, None, 'sp'), may hold values from -0.109375 to 0.109375
- deeper_kernel: bfloat16 [3, 3, 3, 512, 512], P(None, None, None, None, 'sp'), may hold values from -0.078125 to 0.078125
- rise_kernel: bfloat16 [2, 2, 2, 512, 256], replicated, may hold values from -0.375 to 0.375
- decode_kernel: bfloat16 [3, 3, 3, 512, 256], P(None, None, None, 'sp'), may hold values from -0.078125 to 0.078125
- final_kernel: bfloat16 [2, 2, 2, 256, 128], replicated, may hold values from -0.5 to 0.5
Outputs:
- segmented: bfloat16 [128, 16, 16, 128], P(('rep', 'sp')), parts along dimension 0
The draws below stay inside these ranges and needn't reach their ends.
There are 2 independent parts, one for each index of `rep`. The reference program is written for one: setup_inputs(seed, part) draws one part's arguments, and reference() takes and returns one part's arrays. A program takes and returns all parts, laid end to end along the dimension named above; an argument that names none is the same for every part. Nothing has to cross between parts.
All inputs are finite; a program needn't handle non-finite values.
Results may differ from the reference program's by a relative error of at most 0.015.
Values may be sent and summed in bfloat16 or wider, within the bound.
A program may use at most 64 MiB of HBM per device.

```python
import jax
import jax.numpy as jnp
from jax import lax

C1 = 128
C2 = 256
C3 = 512
HT = 16
WD = 16
DEPTH = 64


def draw_volume(key, part):
    fine_key = jax.random.fold_in(key, 11)
    coarse_key = jax.random.fold_in(key, 23)
    coarse_shape = (DEPTH // 4, HT // 4, WD // 4, C1)
    fine = 0.6 * jax.random.normal(fine_key, (DEPTH, HT, WD, C1), jnp.float32)
    coarse = 1.4 * jax.random.normal(coarse_key, coarse_shape, jnp.float32)
    coarse_full = jnp.repeat(jnp.repeat(jnp.repeat(coarse, 4, axis=0), 4, axis=1), 4, axis=2)
    return jnp.clip(fine + coarse_full, -6.0, 6.0).astype(jnp.bfloat16)


def shard_levels(stream_key, extent, pieces, smallest, high):
    factor_of = 1.0
    for dim, shards_of in pieces:
        draws = jax.random.uniform(jax.random.fold_in(jax.random.fold_in(stream_key, 6), dim), (shards_of,), jnp.float32, smallest / len(pieces), high / len(pieces))
        factor_of = factor_of * jnp.repeat(jnp.exp(draws), extent[dim] // shards_of).reshape((-1,) + (1,) * (len(extent) - 1 - dim))
    return factor_of


def noise(rng, shape, deviation, reach, shards=(), held_as=jnp.bfloat16):
    gain = shard_levels(rng, shape, shards, -0.22, 0.18) if shards else 1.0
    values = jax.random.normal(rng, shape, jnp.float32) * deviation * gain
    return jnp.minimum(jnp.maximum(values, -reach), reach).astype(held_as)


def setup_inputs(seed: int = 0, part: int = 0) -> dict:
    seeds = jax.random.split(jax.random.key(seed), 9)
    own_keys = jax.random.split(jax.random.fold_in(seeds[8], part), 9)
    return {
        "volume": draw_volume(jax.random.fold_in(jax.random.fold_in(seeds[8], part), 71), part),
        "first_kernel": noise(seeds[1], (3, 3, 3, C1, C1), (27 * C1 // 2) ** -0.5, 0.15625),
        "second_kernel": noise(seeds[2], (3, 3, 3, C1, C2), (27 * C1 // 2) ** -0.5, 0.15625),
        "deep_kernel": noise(seeds[3], (3, 3, 3, C2, C3), (27 * C2 // 2) ** -0.5, 0.109375, ((4, 16),)),
        "deeper_kernel": noise(seeds[4], (3, 3, 3, C3, C3), (27 * C3 // 2) ** -0.5, 0.078125, ((4, 16),)),
        "rise_kernel": noise(seeds[5], (2, 2, 2, C3, C2), (C3 // 2) ** -0.5, 0.375),
        "decode_kernel": noise(seeds[6], (3, 3, 3, 2 * C2, C2), (27 * C2) ** -0.5, 0.078125, ((3, 16),)),
        "final_kernel": noise(seeds[7], (2, 2, 2, C2, C1), (C2 // 2) ** -0.5, 0.5),
    }


def conv_cube(values, kernel):
    result = lax.conv_general_dilated(values.astype(jnp.float32)[None], kernel.astype(jnp.float32), (1, 1, 1), "SAME", dimension_numbers=("NDHWC", "DHWIO", "NDHWC"), precision=lax.Precision.HIGHEST)
    return result[0]


def pool_mean(values):
    depth, height, width, chans = values.shape
    blocks = values.astype(jnp.float32).reshape(depth // 2, 2, height // 2, 2, width // 2, 2, chans)
    return jnp.mean(blocks, axis=(1, 3, 5)).astype(jnp.bfloat16)


def up_conv(values, kernel):
    depth, height, width, chans = values.shape
    result = jnp.einsum("dhwi,abcio->dahbwco", values.astype(jnp.float32), kernel.astype(jnp.float32), precision=lax.Precision.HIGHEST)
    return result.reshape(2 * depth, 2 * height, 2 * width, kernel.shape[4])


def reference(volume, first_kernel, second_kernel, deep_kernel, deeper_kernel, rise_kernel, decode_kernel, final_kernel):
    first = jax.nn.relu(conv_cube(volume, first_kernel)).astype(jnp.bfloat16)
    pooled_one = pool_mean(first)
    skip = jax.nn.relu(conv_cube(pooled_one, second_kernel)).astype(jnp.bfloat16)
    pooled_two = pool_mean(skip)
    deep = jax.nn.relu(conv_cube(pooled_two, deep_kernel)).astype(jnp.bfloat16)
    deeper = jax.nn.relu(conv_cube(deep, deeper_kernel)).astype(jnp.bfloat16)
    risen = up_conv(deeper, rise_kernel).astype(jnp.bfloat16)
    joined = jnp.concatenate([risen, skip], axis=3)
    decoded = jax.nn.relu(conv_cube(joined, decode_kernel)).astype(jnp.bfloat16)
    return up_conv(decoded, final_kernel).astype(jnp.bfloat16)
```

```python
import functools

import jax
import jax.numpy as jnp
from jax import lax
from jax.experimental import pallas as pl
from jax.experimental.pallas import tpu as pltpu
from jax.sharding import PartitionSpec as P

LANES = 128


def halo_slices(block, axis):
    count = lax.axis_size(axis)
    forward = [(i, i + 1) for i in range(count - 1)]
    backward = [(target, source) for source, target in forward]
    low = lax.ppermute(block[-1:], axis, forward)
    high = lax.ppermute(block[:1], axis, backward)
    return low, high


def with_halo(block, axis):
    low, high = halo_slices(block, axis)
    return jnp.concatenate([low, block, high], axis=0)


def conv_depth(padded, kernel):
    result = lax.conv_general_dilated(
        padded[None],
        kernel,
        (1, 1, 1),
        ((0, 0), (1, 1), (1, 1)),
        dimension_numbers=("NDHWC", "DHWIO", "NDHWC"),
        preferred_element_type=jnp.float32,
    )
    return result[0]


def pool_mean(values):
    depth, height, width, chans = values.shape
    blocks = values.astype(jnp.float32).reshape(depth // 2, 2, height // 2, 2, width // 2, 2, chans)
    return jnp.mean(blocks, axis=(1, 3, 5)).astype(jnp.bfloat16)


def up_conv(values, kernel):
    depth, height, width, chans = values.shape
    result = jnp.einsum("dhwi,abcio->dahbwco", values, kernel, preferred_element_type=jnp.float32)
    return result.reshape(2 * depth, 2 * height, 2 * width, kernel.shape[4])


def conv_rows(values, weight_ref, height, width):
    rows = values.shape[0]
    index = lax.broadcasted_iota(jnp.int32, (rows, 1), 0)
    w_at = index & (width - 1)
    h_at = (index >> (width.bit_length() - 1)) & (height - 1)
    total = jnp.zeros((rows, LANES), jnp.float32)
    for b in range(3):
        for c in range(3):
            shift = width * (b - 1) + (c - 1)
            moved = values if shift == 0 else pltpu.roll(values, (-shift) % rows, 0)
            h_to, w_to = h_at + (b - 1), w_at + (c - 1)
            keep = (h_to >= 0) & (h_to < height) & (w_to >= 0) & (w_to < width)
            moved = jnp.where(keep, moved, 0.0).astype(jnp.bfloat16)
            total += jnp.dot(moved, weight_ref[3 * b + c], preferred_element_type=jnp.float32)
    return total


def bottleneck_kernel(
    n, height, width, part,
    pooled_ref, deep_w_ref, deeper_w_ref, out_ref,
    whole, deep_mine, deep_all, packed,
    send_a, recv_a, send_b, recv_b, send_c, recv_c,
):
    me = lax.axis_index("sp")
    area = height * width
    voxels = n * area
    partner = me + 1 - 2 * (me % 2)
    half = n // 2

    barrier = pltpu.get_barrier_semaphore()

    def greet(k, carry):
        pl.semaphore_signal(
            barrier, inc=1, device_id={"sp": lax.rem(me + k, n)},
            device_id_type=pl.DeviceIdType.MESH,
        )
        return carry

    lax.fori_loop(1, n, greet, 0)
    pl.semaphore_wait(barrier, n - 1)

    def copy_to(src, dst, send_sem, recv_sem, target):
        return pltpu.make_async_remote_copy(
            src_ref=src, dst_ref=dst, send_sem=send_sem, recv_sem=recv_sem,
            device_id={"sp": target}, device_id_type=pl.DeviceIdType.MESH,
        )

    def gather(mine, everyone, send_sem, recv_sem):
        def slot(source):
            return everyone.at[source]

        def direct(k):
            target = lax.rem(me + 2 * k, n)
            return copy_to(mine, slot(me), send_sem.at[k], recv_sem.at[me], target)

        def relay(k):
            source = lax.rem(me + 2 * (half - k), n)
            return copy_to(
                slot(source), slot(source), send_sem.at[half + k], recv_sem.at[source], partner
            )

        def arrival(source):
            return copy_to(mine, slot(source), send_sem.at[0], recv_sem.at[source], partner)

        def start_direct(k, carry):
            direct(k).start()
            return carry

        to_partner = copy_to(mine, slot(me), send_sem.at[0], recv_sem.at[me], partner)
        lax.fori_loop(1, half, start_direct, 0)
        to_partner.start()
        everyone[me] = mine[...]

        def pass_on(k, carry):
            arrival(lax.rem(me + 2 * (half - k), n)).wait_recv()
            relay(k).start()
            return carry

        lax.fori_loop(1, half, pass_on, 0)

        def from_partner(k, carry):
            arrival(lax.rem(partner + 2 * (half - k), n)).wait_recv()
            return carry

        lax.fori_loop(0, half, from_partner, 0)

        def finish():
            to_partner.wait_send()

            def sent(k, carry):
                direct(k).wait_send()
                relay(k).wait_send()
                return carry

            lax.fori_loop(1, half, sent, 0)

        return finish

    finish_a = gather(pooled_ref, whole, send_a, recv_a)
    lanes = lax.broadcasted_iota(jnp.int32, (1, voxels), 1)
    values = whole[...].astype(jnp.float32).reshape(voxels, pooled_ref.shape[1])
    deep = conv_rows(values, deep_w_ref, height, width).T
    below = jnp.where(lanes >= area, pltpu.roll(deep[0:part], area, 1), 0.0)
    above = jnp.where(
        lanes < voxels - area, pltpu.roll(deep[2 * part : 3 * part], voxels - area, 1), 0.0
    )
    deep = below + deep[part : 2 * part] + above
    deep_mine[...] = jnp.maximum(deep, 0.0).astype(jnp.bfloat16)
    finish_b = gather(deep_mine, deep_all, send_b, recv_b)

    values = deep_all[...].astype(jnp.float32).reshape(n * part, voxels).T
    deeper = conv_rows(values, deeper_w_ref, height, width)
    rows = lax.broadcasted_iota(jnp.int32, (voxels, 1), 0)

    def down(block):
        return jnp.where(rows >= area, pltpu.roll(block, area, 0), 0.0)

    def up(block):
        return jnp.where(rows < voxels - area, pltpu.roll(block, voxels - area, 0), 0.0)

    deeper = (
        down(deeper)
        + pltpu.roll(deeper, LANES - part, 1)
        + up(pltpu.roll(deeper, LANES - 2 * part, 1))
    )
    deeper = jnp.maximum(deeper, 0.0)
    lane = lax.broadcasted_iota(jnp.int32, (1, LANES), 1)
    deeper = jnp.where(
        lane < part,
        down(deeper),
        jnp.where(
            lane < 2 * part,
            pltpu.roll(deeper, part, 1),
            up(pltpu.roll(deeper, 2 * part, 1)),
        ),
    )
    packed[...] = deeper.astype(jnp.bfloat16).reshape(n, area, LANES)

    def deal(k):
        target = lax.rem(me + k, n)
        return copy_to(packed.at[target], out_ref.at[me], send_c.at[k], recv_c.at[me], target)

    def start_deal(k, carry):
        deal(k).start()
        return carry

    lax.fori_loop(1, n, start_deal, 0)
    out_ref[me] = packed[me]

    def receive(k, carry):
        source = lax.rem(me + k, n)
        copy_to(
            packed.at[source], out_ref.at[source], send_c.at[k], recv_c.at[source], source
        ).wait_recv()
        return carry

    lax.fori_loop(1, n, receive, 0)

    def sent(k, carry):
        deal(k).wait_send()
        return carry

    lax.fori_loop(1, n, sent, 0)
    finish_a()
    finish_b()


def stack_taps(kernel):
    chans, part = kernel.shape[3], kernel.shape[4]
    stacked = jnp.transpose(kernel, (1, 2, 3, 0, 4)).reshape(9, chans, 3 * part)
    return jnp.pad(stacked, ((0, 0), (0, 0), (0, LANES - 3 * part)))


def bottleneck(pooled, deep_kernel, deeper_kernel):
    n = lax.axis_size("sp")
    _, height, width, chans = pooled.shape
    part = deep_kernel.shape[4]
    area = height * width
    voxels = n * area
    vmem = pl.BlockSpec(memory_space=pltpu.VMEM)
    received = pl.pallas_call(
        functools.partial(bottleneck_kernel, n, height, width, part),
        out_shape=jax.ShapeDtypeStruct((n, area, LANES), jnp.bfloat16),
        in_specs=[vmem] * 3,
        out_specs=vmem,
        scratch_shapes=[
            pltpu.VMEM((n, area, chans), jnp.bfloat16),
            pltpu.VMEM((part, voxels), jnp.bfloat16),
            pltpu.VMEM((n, part, voxels), jnp.bfloat16),
            pltpu.VMEM((n, area, LANES), jnp.bfloat16),
        ]
        + [pltpu.SemaphoreType.DMA((n,))] * 6,
        compiler_params=pltpu.CompilerParams(collective_id=0, has_side_effects=True),
        name="bottleneck",
    )(pooled.reshape(area, chans), stack_taps(deep_kernel), stack_taps(deeper_kernel))
    blocks = received[:, :, : 3 * part].reshape(n, area, 3, part)
    return jnp.transpose(blocks, (2, 1, 0, 3)).reshape(3, height, width, n * part)


def body(
    volume,
    first_kernel,
    second_kernel,
    deep_kernel,
    deeper_kernel,
    rise_kernel,
    decode_kernel,
    final_kernel,
):
    padded_input = with_halo(volume, "sp")
    first = jax.nn.relu(conv_depth(padded_input, first_kernel)).astype(jnp.bfloat16)
    pooled_one = pool_mean(first)
    padded_pool = with_halo(pooled_one, "sp")
    skip = jax.nn.relu(conv_depth(padded_pool, second_kernel)).astype(jnp.bfloat16)
    pooled_two = pool_mean(skip)
    padded_skip = with_halo(skip, "sp")
    deeper_near = bottleneck(pooled_two, deep_kernel, deeper_kernel)
    risen = up_conv(deeper_near, rise_kernel)[1:-1].astype(jnp.bfloat16)
    padded_joined = jnp.concatenate([risen, padded_skip], axis=3)
    whole_decode_kernel = lax.all_gather(decode_kernel, "sp", axis=3, tiled=True)
    decoded = jax.nn.relu(conv_depth(padded_joined, whole_decode_kernel)).astype(jnp.bfloat16)
    return up_conv(decoded, final_kernel).astype(jnp.bfloat16)


def solution(mesh):
    return jax.shard_map(
        body,
        mesh=mesh,
        in_specs=(
            P(("rep", "sp"), None, None, None),
            P(),
            P(),
            P(None, None, None, None, "sp"),
            P(None, None, None, None, "sp"),
            P(),
            P(None, None, None, "sp", None),
            P(),
        ),
        out_specs=P(("rep", "sp"), None, None, None),
        check_vma=False,
    )
```

```python
import functools

import jax
import jax.numpy as jnp
from jax import lax
from jax.experimental import pallas as pl
from jax.experimental.pallas import tpu as pltpu
from jax.sharding import PartitionSpec as P

LANES = 128


def remote(src, dst, send_sem, recv_sem, target):
    return pltpu.make_async_remote_copy(
        src_ref=src, dst_ref=dst, send_sem=send_sem, recv_sem=recv_sem,
        device_id={"sp": target}, device_id_type=pl.DeviceIdType.MESH,
    )


def trade_edges(n, first, last, low, high, send_sem, recv_sem):
    me = lax.axis_index("sp")
    upward = remote(last, low, send_sem.at[0], recv_sem.at[0], lax.rem(me + 1, n))
    downward = remote(first, high, send_sem.at[1], recv_sem.at[1], lax.rem(me + n - 1, n))

    @pl.when(me < n - 1)
    def _():
        upward.start()

    @pl.when(me > 0)
    def _():
        downward.start()

    @pl.when(me == 0)
    def _():
        low[...] = jnp.zeros(low.shape, low.dtype)

    @pl.when(me == n - 1)
    def _():
        high[...] = jnp.zeros(high.shape, high.dtype)

    def finish():
        @pl.when(me > 0)
        def _():
            upward.wait_recv()
            downward.wait_send()

        @pl.when(me < n - 1)
        def _():
            downward.wait_recv()
            upward.wait_send()

    return finish


def greet_neighbours(n):
    me = lax.axis_index("sp")
    barrier = pltpu.get_barrier_semaphore()

    @pl.when(me > 0)
    def _():
        pl.semaphore_signal(
            barrier, inc=1, device_id={"sp": lax.rem(me + n - 1, n)},
            device_id_type=pl.DeviceIdType.MESH,
        )

    @pl.when(me < n - 1)
    def _():
        pl.semaphore_signal(
            barrier, inc=1, device_id={"sp": lax.rem(me + 1, n)},
            device_id_type=pl.DeviceIdType.MESH,
        )

    @pl.when((me > 0) & (me < n - 1))
    def _():
        pl.semaphore_wait(barrier, 2)

    @pl.when((me == 0) | (me == n - 1))
    def _():
        pl.semaphore_wait(barrier, 1)


def first_level_kernel(
    n, depth, height, width,
    volume_ref, weight_ref, out_ref,
    ends, taps, sums, send_a, recv_a, send_b, recv_b,
):
    area = height * width
    chans = volume_ref.shape[2]
    greet_neighbours(n)
    finish = trade_edges(
        n, volume_ref.at[0], volume_ref.at[depth - 1], ends.at[0], ends.at[1], send_a, recv_a
    )
    index = lax.broadcasted_iota(jnp.int32, (area, 1), 0) & (width - 1)
    blank = jnp.zeros((depth + 2, width, 3 * chans), jnp.bfloat16)
    taps[:, 0:width] = blank
    taps[:, area + width : area + 2 * width] = blank

    def spread(at, values):
        taps[at, width : area + width, chans : 2 * chans] = values
        values = values.astype(jnp.float32)
        left = jnp.where(index > 0, pltpu.roll(values, 1, 0), 0.0)
        right = jnp.where(index < width - 1, pltpu.roll(values, area - 1, 0), 0.0)
        taps[at, width : area + width, 0:chans] = left.astype(jnp.bfloat16)
        taps[at, width : area + width, 2 * chans : 3 * chans] = right.astype(jnp.bfloat16)

    for d in range(depth):
        spread(d + 1, volume_ref[d])
    finish()
    spread(0, ends[0])
    spread(depth + 1, ends[1])
    for pair in range(depth // 2):
        total = jnp.zeros((2 * area, weight_ref.shape[3]), jnp.float32)
        for a in range(3):
            for b in range(3):
                block = taps[2 * pair + a : 2 * pair + a + 2, b * width : b * width + area]
                total += jnp.dot(
                    block.reshape(2 * area, 3 * chans), weight_ref[a, b],
                    preferred_element_type=jnp.float32,
                )
        total = jnp.maximum(total, 0.0).astype(jnp.bfloat16).astype(jnp.float32)
        total = total[0:area] + total[area : 2 * area]
        total = total.reshape(height // 2, 2, width, total.shape[1]).sum(axis=1)
        sums[...] = total.reshape(area // 2, total.shape[2])
        total = sums[pl.ds(0, area // 4, 2), :] + sums[pl.ds(1, area // 4, 2), :]
        out_ref[1 + pair] = (total * 0.125).astype(jnp.bfloat16)
    halves = depth // 2
    trade_edges(
        n, out_ref.at[1], out_ref.at[halves], out_ref.at[0], out_ref.at[halves + 1],
        send_b, recv_b,
    )()


def first_level(volume, kernel):
    n = lax.axis_size("sp")
    depth, height, width, chans = volume.shape
    outs = kernel.shape[4]
    area = height * width
    vmem = pl.BlockSpec(memory_space=pltpu.VMEM)
    padded = pl.pallas_call(
        functools.partial(first_level_kernel, n, depth, height, width),
        out_shape=jax.ShapeDtypeStruct((depth // 2 + 2, area // 4, outs), jnp.bfloat16),
        in_specs=[vmem] * 2,
        out_specs=vmem,
        scratch_shapes=[
            pltpu.VMEM((2, area, chans), jnp.bfloat16),
            pltpu.VMEM((depth + 2, area + 2 * width, 3 * chans), jnp.bfloat16),
            pltpu.VMEM((area // 2, outs), jnp.float32),
        ]
        + [pltpu.SemaphoreType.DMA((2,))] * 4,
        compiler_params=pltpu.CompilerParams(
            collective_id=1, has_side_effects=True, vmem_limit_bytes=16 << 20
        ),
        name="first_level",
    )(volume.reshape(depth, area, chans), kernel.reshape(3, 3, 3 * chans, outs))
    return padded.reshape(depth // 2 + 2, height // 2, width // 2, outs)


def conv_depth(padded, kernel):
    result = lax.conv_general_dilated(
        padded[None],
        kernel,
        (1, 1, 1),
        ((0, 0), (1, 1), (1, 1)),
        dimension_numbers=("NDHWC", "DHWIO", "NDHWC"),
        preferred_element_type=jnp.float32,
    )
    return result[0]


def pool_mean(values):
    depth, height, width, chans = values.shape
    blocks = values.astype(jnp.float32).reshape(depth // 2, 2, height // 2, 2, width // 2, 2, chans)
    return jnp.mean(blocks, axis=(1, 3, 5)).astype(jnp.bfloat16)


def up_conv(values, kernel):
    depth, height, width, chans = values.shape
    result = jnp.einsum("dhwi,abcio->dahbwco", values, kernel, preferred_element_type=jnp.float32)
    return result.reshape(2 * depth, 2 * height, 2 * width, kernel.shape[4])


def conv_rows(values, weight_ref, height, width):
    rows = values.shape[0]
    index = lax.broadcasted_iota(jnp.int32, (rows, 1), 0)
    w_at = index & (width - 1)
    h_at = (index >> (width.bit_length() - 1)) & (height - 1)
    part, chans = weight_ref.shape[2:]
    blank = jnp.zeros((LANES - 3 * part, chans), weight_ref.dtype)
    total = jnp.zeros((rows, LANES), jnp.float32)
    for b in range(3):
        for c in range(3):
            shift = width * (b - 1) + (c - 1)
            moved = values if shift == 0 else pltpu.roll(values, (-shift) % rows, 0)
            h_to, w_to = h_at + (b - 1), w_at + (c - 1)
            keep = (h_to >= 0) & (h_to < height) & (w_to >= 0) & (w_to < width)
            moved = jnp.where(keep, moved, 0.0).astype(jnp.bfloat16)
            tap = 3 * b + c
            weight = jnp.concatenate([weight_ref[a, tap] for a in range(3)] + [blank], axis=0)
            total += lax.dot_general(
                moved, weight, (((1,), (1,)), ((), ())), preferred_element_type=jnp.float32
            )
    return total


def bottleneck_kernel(
    n, height, width, part,
    pooled_ref, skip_ref, deep_w_ref, deeper_w_ref, out_ref, near_ref,
    whole, deep_mine, deep_all, packed,
    send_a, recv_a, send_b, recv_b, send_c, recv_c, send_d, recv_d,
):
    me = lax.axis_index("sp")
    area = height * width
    voxels = n * area
    partner = me + 1 - 2 * (me % 2)
    half = n // 2

    barrier = pltpu.get_barrier_semaphore()

    def greet(k, carry):
        pl.semaphore_signal(
            barrier, inc=1, device_id={"sp": lax.rem(me + k, n)},
            device_id_type=pl.DeviceIdType.MESH,
        )
        return carry

    lax.fori_loop(1, n, greet, 0)
    pl.semaphore_wait(barrier, n - 1)

    def gather(mine, everyone, send_sem, recv_sem):
        def slot(source):
            return everyone.at[source]

        def direct(k):
            target = lax.rem(me + 2 * k, n)
            return remote(mine, slot(me), send_sem.at[k], recv_sem.at[me], target)

        def relay(k):
            source = lax.rem(me + 2 * (half - k), n)
            return remote(
                slot(source), slot(source), send_sem.at[half + k], recv_sem.at[source], partner
            )

        def arrival(source):
            return remote(mine, slot(source), send_sem.at[0], recv_sem.at[source], partner)

        def start_direct(k, carry):
            direct(k).start()
            return carry

        to_partner = remote(mine, slot(me), send_sem.at[0], recv_sem.at[me], partner)
        lax.fori_loop(1, half, start_direct, 0)
        to_partner.start()
        everyone[me] = mine[...]

        def pass_on(k, carry):
            arrival(lax.rem(me + 2 * (half - k), n)).wait_recv()
            relay(k).start()
            return carry

        lax.fori_loop(1, half, pass_on, 0)

        def from_partner(k, carry):
            arrival(lax.rem(partner + 2 * (half - k), n)).wait_recv()
            return carry

        lax.fori_loop(0, half, from_partner, 0)

        def finish():
            to_partner.wait_send()

            def sent(k, carry):
                direct(k).wait_send()
                relay(k).wait_send()
                return carry

            lax.fori_loop(1, half, sent, 0)

        return finish

    finish_a = gather(pooled_ref, whole, send_a, recv_a)
    depth = skip_ref.shape[0]
    finish_d = trade_edges(
        n, skip_ref.at[0], skip_ref.at[depth - 1], near_ref.at[0], near_ref.at[1], send_d, recv_d
    )
    lanes = lax.broadcasted_iota(jnp.int32, (1, voxels), 1)
    values = whole[...].astype(jnp.float32).reshape(voxels, pooled_ref.shape[1])
    deep = conv_rows(values, deep_w_ref, height, width).T
    below = jnp.where(lanes >= area, pltpu.roll(deep[0:part], area, 1), 0.0)
    above = jnp.where(
        lanes < voxels - area, pltpu.roll(deep[2 * part : 3 * part], voxels - area, 1), 0.0
    )
    deep = below + deep[part : 2 * part] + above
    deep_mine[...] = jnp.maximum(deep, 0.0).astype(jnp.bfloat16)
    finish_b = gather(deep_mine, deep_all, send_b, recv_b)

    values = deep_all[...].astype(jnp.float32).reshape(n * part, voxels).T
    deeper = conv_rows(values, deeper_w_ref, height, width)
    rows = lax.broadcasted_iota(jnp.int32, (voxels, 1), 0)

    def down(block):
        return jnp.where(rows >= area, pltpu.roll(block, area, 0), 0.0)

    def up(block):
        return jnp.where(rows < voxels - area, pltpu.roll(block, voxels - area, 0), 0.0)

    deeper = (
        down(deeper)
        + pltpu.roll(deeper, LANES - part, 1)
        + up(pltpu.roll(deeper, LANES - 2 * part, 1))
    )
    deeper = jnp.maximum(deeper, 0.0)
    lane = lax.broadcasted_iota(jnp.int32, (1, LANES), 1)
    deeper = jnp.where(
        lane < part,
        down(deeper),
        jnp.where(
            lane < 2 * part,
            pltpu.roll(deeper, part, 1),
            up(pltpu.roll(deeper, 2 * part, 1)),
        ),
    )
    packed[...] = deeper.astype(jnp.bfloat16).reshape(n, area, LANES)

    def deal(k):
        target = lax.rem(me + k, n)
        return remote(packed.at[target], out_ref.at[me], send_c.at[k], recv_c.at[me], target)

    def start_deal(k, carry):
        deal(k).start()
        return carry

    lax.fori_loop(1, n, start_deal, 0)
    out_ref[me] = packed[me]

    def receive(k, carry):
        source = lax.rem(me + k, n)
        remote(
            packed.at[source], out_ref.at[source], send_c.at[k], recv_c.at[source], source
        ).wait_recv()
        return carry

    lax.fori_loop(1, n, receive, 0)

    def sent(k, carry):
        deal(k).wait_send()
        return carry

    lax.fori_loop(1, n, sent, 0)
    finish_a()
    finish_b()
    finish_d()


def out_major(kernel):
    chans, part = kernel.shape[3], kernel.shape[4]
    return jnp.transpose(kernel, (0, 1, 2, 4, 3)).reshape(3, 9, part, chans)


def bottleneck(pooled, skip, deep_kernel, deeper_kernel):
    n = lax.axis_size("sp")
    _, height, width, chans = pooled.shape
    part = deep_kernel.shape[4]
    area = height * width
    voxels = n * area
    vmem = pl.BlockSpec(memory_space=pltpu.VMEM)
    received, near = pl.pallas_call(
        functools.partial(bottleneck_kernel, n, height, width, part),
        out_shape=(
            jax.ShapeDtypeStruct((n, area, LANES), jnp.bfloat16),
            jax.ShapeDtypeStruct((2,) + skip.shape[1:], jnp.bfloat16),
        ),
        in_specs=[vmem] * 4,
        out_specs=(vmem, vmem),
        scratch_shapes=[
            pltpu.VMEM((n, area, chans), jnp.bfloat16),
            pltpu.VMEM((part, voxels), jnp.bfloat16),
            pltpu.VMEM((n, part, voxels), jnp.bfloat16),
            pltpu.VMEM((n, area, LANES), jnp.bfloat16),
        ]
        + [pltpu.SemaphoreType.DMA((n,))] * 6
        + [pltpu.SemaphoreType.DMA((2,))] * 2,
        compiler_params=pltpu.CompilerParams(
            collective_id=0, has_side_effects=True, vmem_limit_bytes=24 << 20
        ),
        name="bottleneck",
    )(pooled.reshape(area, chans), skip, out_major(deep_kernel), out_major(deeper_kernel))
    blocks = received[:, :, : 3 * part].reshape(n, area, 3, part)
    return jnp.transpose(blocks, (2, 1, 0, 3)).reshape(3, height, width, n * part), near


def body(
    volume,
    first_kernel,
    second_kernel,
    deep_kernel,
    deeper_kernel,
    rise_kernel,
    decode_kernel,
    final_kernel,
):
    padded_pool = first_level(volume, first_kernel)
    skip = jax.nn.relu(conv_depth(padded_pool, second_kernel)).astype(jnp.bfloat16)
    pooled_two = pool_mean(skip)
    deeper_near, skip_near = bottleneck(pooled_two, skip, deep_kernel, deeper_kernel)
    padded_skip = jnp.concatenate([skip_near[:1], skip, skip_near[1:]], axis=0)
    risen = up_conv(deeper_near, rise_kernel)[1:-1].astype(jnp.bfloat16)
    padded_joined = jnp.concatenate([risen, padded_skip], axis=3)
    whole_decode_kernel = lax.all_gather(decode_kernel, "sp", axis=3, tiled=True)
    decoded = jax.nn.relu(conv_depth(padded_joined, whole_decode_kernel)).astype(jnp.bfloat16)
    return up_conv(decoded, final_kernel).astype(jnp.bfloat16)


def solution(mesh):
    return jax.shard_map(
        body,
        mesh=mesh,
        in_specs=(
            P(("rep", "sp"), None, None, None),
            P(),
            P(),
            P(None, None, None, None, "sp"),
            P(None, None, None, None, "sp"),
            P(),
            P(None, None, None, "sp", None),
            P(),
        ),
        out_specs=P(("rep", "sp"), None, None, None),
        check_vma=False,
    )
```
